32 devices in a mesh: batch: 4 (over y, x), lat: 8 (over z, core).
Axes of the slice: x: 2, y: 2, z: 4, core: 2. Of those that a mesh axis runs over, the one named last changes fastest.
Arguments:
- patches: bfloat16 [8, 1024, 384], P('batch', 'lat'), may hold values from -6 to 6
- levels: int32 [8, 1024], P('batch', 'lat'), may hold values from 5 to 13, as said below
- lead_index: int32 [8], P('batch'), may hold values from 0 to 7
- lead_table: bfloat16 [8, 384], P('batch', 'lat'), may hold values from -5 to 5
- ada_weight: bfloat16 [2, 384, 2304], P(None, 'lat', 'batch'), may hold values from -0.3125 to 0.3125
- qkv_weight: bfloat16 [2, 384, 1152], P(None, 'lat', 'batch'), may hold values from -0.3125 to 0.3125
- out_weight: bfloat16 [2, 384, 384], P(None, 'lat', 'batch'), may hold values from -6 to 6
- up_weight: bfloat16 [2, 384, 1536], P(None, 'lat', 'batch'), may hold values from -0.3125 to 0.3125
- down_weight: bfloat16 [2, 1536, 384], P(None, 'lat', 'batch'), may hold values from -0.15625 to 0.15625
- cotangent: bfloat16 [8, 1024, 384], P('batch', 'lat'), may hold values from -6 to 6
Outputs:
- output: bfloat16 [8, 1024, 384], P('batch', 'lat')
- patches_grad: bfloat16 [8, 1024, 384], P('batch', 'lat')
- table_grad: float32 [8, 384], P('batch', 'lat')
- ada_grad: float32 [2, 384, 2304], P(None, 'lat', 'batch')
- qkv_grad: float32 [2, 384, 1152], P(None, 'lat', 'batch')
- out_grad: float32 [2, 384, 384], P(None, 'lat', 'batch')
- up_grad: float32 [2, 384, 1536], P(None, 'lat', 'batch')
- down_grad: float32 [2, 1536, 384], P(None, 'lat', 'batch')
The draws below stay inside these ranges and needn't reach their ends.
Inputs may be any that keep to these rules, and one draw needn't show every extreme that they name: Patches among the first and last 128 positions of an item have at most 8 levels; every item has a patch with 5 and one with 13.
All inputs are finite; a program needn't handle non-finite values.
Results may differ from the reference program's by a relative error of at most 0.025.
Values may be sent and summed in bfloat16 or wider, within the bound.
No kernel may reach another device: no remote copies, remote signals or barrier semaphores. Data moves between devices by JAX's collectives and lax.ppermute only.
A program may use at most 192 MiB of HBM per device.

```python
import jax
import jax.numpy as jnp
from jax import lax

D = 384
HEADS = 6
HEAD_DIM = 64
FF = 1536
LEADS = 8
LAYERS = 2
SEQ = 1024
ITEMS = 8


def draw_levels(key, part):
    counts = jax.random.randint(key, (ITEMS, SEQ), 5, 14)
    place = jnp.arange(SEQ, dtype=jnp.int32)
    polar = (place < SEQ // 8) | (place >= SEQ - SEQ // 8)
    counts = jnp.where(polar[None, :], jnp.minimum(counts, 8), counts)
    counts = counts.at[:, 0].set(5)
    counts = counts.at[:, SEQ // 2].set(13)
    return counts.astype(jnp.int32)


def place_ends(values, own_key, low, high):
    spot = [jax.random.randint(jax.random.fold_in(own_key, axis), (), 0, length) for axis, length in enumerate(values.shape)]
    longest = values.shape.index(max(values.shape))
    neighbour = spot[:longest] + [(spot[longest] + 1) % values.shape[longest]] + spot[longest + 1:]
    return values.at[tuple(spot)].set(low).at[tuple(neighbour)].set(high)


def block_scale(rng, dims, shards, smallest, top_value):
    factor_of, own = 1.0, jax.random.fold_in(rng, 6)
    for position, shards_of in shards:
        steps = jnp.exp(jax.random.uniform(jax.random.fold_in(own, position), (shards_of,), jnp.float32, smallest / len(shards), top_value / len(shards)))
        factor_of = factor_of * jnp.repeat(steps, dims[position] // shards_of).reshape([-1 if axis == position else 1 for axis in range(len(dims))])
    return factor_of


def scatter_about(rng, extent, deviation, reach, shards=(), kind=jnp.bfloat16):
    values = deviation * jax.random.normal(rng, extent, jnp.float32)
    if shards:
        values = values * block_scale(rng, extent, shards, -0.22, 0.18)
    return jnp.clip(values, -reach, reach).astype(kind)


def setup_inputs(seed: int = 0) -> dict:
    key_list = jax.random.split(jax.random.key(seed), 11)
    patches = scatter_about(key_list[0], (ITEMS, SEQ, D), 1.0, 6.0, ((0, 4), (1, 8)))
    levels = draw_levels(jax.random.fold_in(key_list[10], 71), 0)
    lead_index = place_ends(jax.random.randint(key_list[2], (ITEMS,), 0, LEADS), jax.random.fold_in(key_list[2], 1), 0, LEADS - 1).astype(jnp.int32)
    lead_table = scatter_about(key_list[3], (LEADS, D), 1.0, 5.0, ((0, 4), (1, 8)))
    ada_weight = scatter_about(key_list[4], (LAYERS, D, 6 * D), D ** -0.5, 0.3125, ((1, 8), (2, 4)))
    qkv_weight = scatter_about(key_list[5], (LAYERS, D, 3 * D), D ** -0.5, 0.3125, ((1, 8), (2, 4)))
    out_weight = scatter_about(key_list[6], (LAYERS, D, D), (max(1, 2 * D // SEQ)) ** -0.5, 6.0, ((1, 8), (2, 4)))
    up_weight = scatter_about(key_list[7], (LAYERS, D, FF), D ** -0.5, 0.3125, ((1, 8), (2, 4)))
    down_weight = scatter_about(key_list[8], (LAYERS, FF, D), FF ** -0.5, 0.15625, ((1, 8), (2, 4)))
    cotangent = scatter_about(key_list[9], (ITEMS, SEQ, D), 1.0, 6.0, ((0, 4), (1, 8)))
    return dict(patches=patches, levels=levels, lead_index=lead_index, lead_table=lead_table, ada_weight=ada_weight, qkv_weight=qkv_weight, out_weight=out_weight, up_weight=up_weight, down_weight=down_weight, cotangent=cotangent)


@jax.custom_vjp
def low(v):
    return lax.optimization_barrier(v.astype(jnp.bfloat16)).astype(jnp.float32)

@jax.custom_vjp
def low_back(v):
    return v

def low_keep(v):
    return (low(v), None)

def low_pass(kept, grad):
    return (grad,)

def back_keep(v):
    return (v, None)

def back_low(kept, grad):
    return (low(grad),)
low.defvjp(low_keep, low_pass)
low_back.defvjp(back_keep, back_low)
eps = 1e-06
masked_score = -1e+30
needed_levels = 9
highest = lax.Precision.HIGHEST

def layer_norm(stream):
    center = stream - lax.optimization_barrier(jnp.mean(stream, axis=-1, keepdims=True))
    spread = lax.optimization_barrier(jnp.mean(center * center, axis=-1, keepdims=True))
    return center * lax.rsqrt(spread + eps)

def matmul(left, right):
    return jnp.dot(left, right, precision=highest, preferred_element_type=jnp.float32)

def attend(queries, key_rows, value_rows, valid):
    total_rows = queries.shape[0]
    block_rows = 512 if total_rows % 512 == 0 else total_rows
    number = total_rows // block_rows
    score_scale = HEAD_DIM ** (-0.5)
    query_blocks = queries.reshape(number, block_rows, HEADS, HEAD_DIM)
    key_heads = key_rows.reshape(total_rows, HEADS, HEAD_DIM)
    value_heads = value_rows.reshape(total_rows, HEADS, HEAD_DIM)
    starts = jnp.arange(number, dtype=jnp.int32) * block_rows
    key_pos = jnp.arange(total_rows, dtype=jnp.int32)

    def one_block(operands):
        query_block, first_row = operands
        score = low_back(jnp.einsum('qhd,khd->hqk', query_block, key_heads, precision=highest) * score_scale)
        query_pos = first_row + jnp.arange(block_rows, dtype=jnp.int32)
        permit = ((valid[None, :] > 0.5) | (query_pos[:, None] == key_pos[None, :]))[None]
        score = jnp.where(permit, score, masked_score)
        top_score = lax.optimization_barrier(jnp.max(score, axis=-1, keepdims=True))
        exp_score = jnp.exp(score - top_score)
        prob = exp_score / lax.optimization_barrier(jnp.sum(exp_score, axis=-1, keepdims=True))
        return jnp.einsum('hqk,khd->qhd', low(prob), value_heads, precision=highest)
    mixed = lax.map(jax.checkpoint(one_block), (query_blocks, starts))
    return mixed.reshape(total_rows, D)

def one_item(stream, cond, valid, ada_weight, qkv_weight, out_weight, up_weight, down_weight):
    for layer_number in range(LAYERS):
        modulation = matmul(cond[None, :], ada_weight[layer_number])[0]
        shift_one = modulation[0:D]
        scale_one = modulation[D:2 * D]
        gate_one = modulation[2 * D:3 * D]
        shift_two = modulation[3 * D:4 * D]
        scale_two = modulation[4 * D:5 * D]
        gate_two = modulation[5 * D:6 * D]
        attn_in = low(layer_norm(stream) * (1.0 + scale_one) + shift_one)
        qkv = low(low_back(matmul(attn_in, qkv_weight[layer_number])))
        attn_mix = attend(qkv[:, :D], qkv[:, D:2 * D], qkv[:, 2 * D:], valid)
        branch_one = low_back(matmul(low(low_back(attn_mix)), out_weight[layer_number]))
        stream = stream + gate_one * branch_one
        mlp_in = low(layer_norm(stream) * (1.0 + scale_two) + shift_two)
        up_proj = low_back(matmul(mlp_in, up_weight[layer_number]))
        gelu_low = low(jax.nn.gelu(up_proj, approximate=True))
        branch_two = low_back(matmul(gelu_low, down_weight[layer_number]))
        stream = stream + gate_two * branch_two
    return stream

def forward(patches, lead_table, ada_weight, qkv_weight, out_weight, up_weight, down_weight, lead_hot, valid):
    cond = low(jax.nn.silu(matmul(lead_hot, lead_table)))

    def per_item(operands):
        return one_item(operands[0], operands[1], operands[2], ada_weight, qkv_weight, out_weight, up_weight, down_weight)
    return lax.map(per_item, (patches, cond, valid))

def reference(patches, levels, lead_index, lead_table, ada_weight, qkv_weight, out_weight, up_weight, down_weight, cotangent):
    lead_hot = (lead_index[:, None] == jnp.arange(LEADS, dtype=jnp.int32)[None, :]).astype(jnp.float32)
    valid = (levels >= needed_levels).astype(jnp.float32)

    def func(patch_in, table_in, ada_in, qkv_in, out_in, up_in, down_in):
        return forward(patch_in, table_in, ada_in, qkv_in, out_in, up_in, down_in, lead_hot, valid)
    result, pull = jax.vjp(func, patches.astype(jnp.float32), lead_table.astype(jnp.float32), ada_weight.astype(jnp.float32), qkv_weight.astype(jnp.float32), out_weight.astype(jnp.float32), up_weight.astype(jnp.float32), down_weight.astype(jnp.float32))
    grads = pull(cotangent.astype(jnp.float32))
    return (result.astype(jnp.bfloat16), grads[0].astype(jnp.bfloat16), grads[1], grads[2], grads[3], grads[4], grads[5], grads[6])
```

```python
import math

import jax
import jax.numpy as jnp
from jax import lax
from jax.sharding import PartitionSpec as P

HEADS = 6
eps = 1e-06
masked_score = -1e30
needed_levels = 9
highest = lax.Precision.HIGHEST
bf16 = jnp.bfloat16
f32 = jnp.float32


def layer_norm(stream):
    center = stream - jnp.mean(stream, axis=-1, keepdims=True)
    spread = jnp.mean(center * center, axis=-1, keepdims=True)
    return center * lax.rsqrt(spread + eps)


def norm_back(stream, upstream):
    return jax.vjp(layer_norm, stream)[1](upstream)[0]


def gelu_tanh(values):
    return jax.nn.gelu(values, approximate=True)


def gelu_back(values, upstream):
    return jax.vjp(gelu_tanh, values)[1](upstream)[0]


def low_dot(left, right):
    return jnp.dot(left, right, preferred_element_type=f32)


def dot_first(left, right):
    return lax.dot_general(left, right, (((0,), (0,)), ((), ())), preferred_element_type=f32)


def dot_second(left, right):
    return lax.dot_general(left, right, (((1,), (1,)), ((), ())), preferred_element_type=f32)


class Bits:
    def __init__(self, batch, lat, items):
        group = lat // items
        self.batch, self.lat, self.items, self.group = batch, lat, items, group
        self.core = ("lat", 1, lat)
        self.zs = [("lat", 1 << k, lat) for k in range(1, group.bit_length() - 1)]
        self.item = [("lat", group << k, lat) for k in range(items.bit_length() - 1)]
        self.bs = [("batch", 1 << k, batch) for k in range(batch.bit_length() - 1)]


def swap(array, stage):
    name, mask, size = stage
    return lax.ppermute(array, name, [(i, i ^ mask) for i in range(size)])


def gather(array, stages):
    held = array[None]
    for stage in stages:
        held = jnp.concatenate([held, swap(held, stage)], axis=0)
    return held


def scatter(array, stages):
    for stage in reversed(stages):
        half = array.shape[0] // 2
        got = swap(array[half:], stage)
        array = (array[:half].astype(f32) + got.astype(f32)).astype(array.dtype)
    return array[0]


def spread(array, stages):
    held = array[:, None]
    for stage in reversed(stages):
        half = held.shape[0] // 2
        got = swap(held[half:], stage)
        held = jnp.stack([held[:half], got], axis=2)
        held = held.reshape((half, -1) + held.shape[3:])
    return held[0]


def slot_bits(position, stages, name):
    total = 0
    for place, (axis, mask, size) in enumerate(stages):
        if axis == name:
            total = total + jnp.where((position & mask) != 0, 1 << place, 0)
    return total


def slot_order(stages, bits):
    lat_far = jnp.arange(bits.lat, dtype=jnp.int32) ^ lax.axis_index("lat")
    batch_far = jnp.arange(bits.batch, dtype=jnp.int32) ^ lax.axis_index("batch")
    return (
        slot_bits(lat_far, stages, "lat")[:, None] + slot_bits(batch_far, stages, "batch")[None, :]
    )


def unpack(held, order, rows, columns):
    lat, batch = order.shape
    picked = jnp.take(held, order.reshape(-1), axis=0).reshape(lat, batch, rows, columns)
    return picked.transpose(0, 2, 1, 3).reshape(lat * rows, batch * columns)


def pack(whole, order, rows, columns):
    lat, batch = order.shape
    split = whole.reshape(lat, rows, batch, columns).transpose(0, 2, 1, 3)
    split = split.reshape(lat * batch, rows, columns)
    back = jnp.argsort(order.reshape(-1))
    return jnp.take(split, back, axis=0)


def heads_of(matrix):
    rows, width = matrix.shape
    return matrix.reshape(rows, HEADS, width // HEADS).transpose(1, 0, 2)


def rows_of(heads):
    count, rows, dim = heads.shape
    return heads.transpose(1, 0, 2).reshape(rows, count * dim)


def attend(query, keys, values, permit):
    scale = 1.0 / math.sqrt(query.shape[-1])
    score = jnp.einsum("hqd,hkd->hqk", query, keys, preferred_element_type=f32) * scale
    score = jnp.where(permit[None], score, masked_score)
    top = jnp.max(score, axis=-1, keepdims=True)
    expo = jnp.exp(score - top)
    total = jnp.sum(expo, axis=-1, keepdims=True)
    mix = jnp.einsum("hqk,hkd->hqd", expo.astype(bf16), values, preferred_element_type=f32) / total
    return mix, (top + jnp.log(total))


def attend_back(query, keys, values, permit, mix, lse, grad):
    scale = 1.0 / math.sqrt(query.shape[-1])
    score = jnp.einsum("hqd,hkd->hqk", query, keys, preferred_element_type=f32) * scale
    prob = jnp.where(permit[None], jnp.exp(score - lse), 0.0)
    delta = jnp.sum(grad.astype(f32) * mix, axis=-1, keepdims=True)
    d_prob = jnp.einsum("hqd,hkd->hqk", grad, values, preferred_element_type=f32)
    d_score = (prob * (d_prob - delta)).astype(bf16)
    d_v = jnp.einsum("hqk,hqd->hkd", prob.astype(bf16), grad, preferred_element_type=f32)
    d_k = jnp.einsum("hqk,hqd->hkd", d_score, query, preferred_element_type=f32) * scale
    d_q = jnp.einsum("hqk,hkd->hqd", d_score, keys, preferred_element_type=f32) * scale
    return d_q, d_k, d_v


def take_own(array, bits):
    return lax.dynamic_index_in_dim(array, lax.axis_index("lat") // bits.group, 0, keepdims=False)


def item_rows(array, bits):
    mine = lax.axis_index("lat") // bits.group
    parts = []
    for far in range(bits.items):
        part = lax.dynamic_index_in_dim(array, mine ^ far, 0, keepdims=False)
        if far:
            part = swap(part, ("lat", far * bits.group, bits.lat))
        parts.append(part)
    return jnp.concatenate(parts, axis=0)


def band_rows(array, bits):
    mine = lax.axis_index("lat") // bits.group
    rows = array.shape[0] // bits.items
    parts = []
    for far in range(bits.items):
        part = array[far * rows : (far + 1) * rows]
        if far:
            part = swap(part, ("lat", far * bits.group, bits.lat))
        parts.append(part)
    stacked = jnp.stack(parts)
    order = jnp.arange(bits.items, dtype=jnp.int32) ^ mine
    return jnp.take(stacked, order, axis=0)


def per_device(bits, patches, levels, lead_index, lead_table, ada, qkv, out, up, down, cotangent):
    layers = qkv.shape[0]
    width = patches.shape[2]
    lat_at, batch_at = lax.axis_index("lat"), lax.axis_index("batch")
    mine = lat_at // bits.group
    full = bits.zs + bits.item + bits.bs + [bits.core]
    order = slot_order(full, bits)

    shards = (qkv, out, up, down)
    whole = [
        [
            unpack(gather(shard[layer], full), order, shard.shape[1], shard.shape[2])
            for shard in shards
        ]
        for layer in range(layers)
    ]

    table_rows, lat_cols = lead_table.shape
    lead_row = jnp.broadcast_to(lead_index.astype(f32)[None], (table_rows, bits.items))
    lead_row = jnp.concatenate([lead_table.astype(f32), lead_row], axis=1)
    got = gather(lead_row, bits.bs)
    batch_far = jnp.arange(bits.batch, dtype=jnp.int32)
    row_ids = ((batch_at ^ batch_far)[:, None] * table_rows + jnp.arange(table_rows)[None]).reshape(-1)
    table = got[:, :, :lat_cols].reshape(-1, lat_cols)
    leads = got[:, 0, lat_cols:].reshape(-1)
    hot = (leads[:, None] == row_ids[None, :].astype(f32)).astype(f32)
    embed = jnp.dot(hot, table, precision=highest)
    cond = jax.nn.silu(embed).astype(bf16)
    part = jnp.stack([low_dot(cond, ada[layer]) for layer in range(layers)], axis=1)
    columns = part.shape[-1]
    part = part.reshape(bits.batch, bits.items, layers, columns)
    part = jnp.take(part, mine ^ jnp.arange(bits.items, dtype=jnp.int32), axis=1)
    part = part.transpose(1, 0, 2, 3)
    part = scatter(part, bits.item)
    for stage in bits.zs + [bits.core]:
        part = part + swap(part, stage)
    part = spread(part, bits.bs)
    part = jnp.take(part, batch_at ^ jnp.arange(bits.batch, dtype=jnp.int32), axis=0)
    modulation = part.transpose(1, 0, 2).reshape(layers, 6, width)

    rows = item_rows(patches, bits)
    flags = item_rows((levels >= needed_levels).astype(bf16), bits)
    upstream = item_rows(cotangent, bits).astype(f32)
    near = bits.zs + [bits.core]
    key_flags = gather(flags, near).reshape(-1)
    count = rows.shape[0]
    place = jnp.arange(key_flags.shape[0], dtype=jnp.int32)
    permit = (key_flags[None, :] > 0.5) | (place[None, :] == jnp.arange(count)[:, None])

    stream = rows.astype(f32)
    saved = []
    for layer in range(layers):
        w_qkv, w_out, w_up, w_down = whole[layer]
        shift1, scale1, gate1, shift2, scale2, gate2 = [modulation[layer, k] for k in range(6)]
        attn_in = (layer_norm(stream) * (1.0 + scale1) + shift1).astype(bf16)
        qkv_rows = low_dot(attn_in, w_qkv).astype(bf16)
        pairs = gather(qkv_rows[:, width:], near).reshape(-1, 2 * width)
        query = heads_of(qkv_rows[:, :width])
        keys, values = heads_of(pairs[:, :width]), heads_of(pairs[:, width:])
        mix, lse = attend(query, keys, values, permit)
        attn_low = rows_of(mix).astype(bf16)
        branch1 = low_dot(attn_low, w_out)
        middle = stream + gate1 * branch1
        mlp_in = (layer_norm(middle) * (1.0 + scale2) + shift2).astype(bf16)
        up_proj = low_dot(mlp_in, w_up)
        gelu_low = gelu_tanh(up_proj).astype(bf16)
        branch2 = low_dot(gelu_low, w_down)
        result = middle + gate2 * branch2
        saved.append((stream, attn_in, query, keys, values, mix, lse, attn_low, branch1, middle, mlp_in, up_proj, gelu_low, branch2))
        stream = result
    output = band_rows(stream.astype(bf16), bits)

    grads = [None] * layers
    mods = [None] * layers
    for layer in reversed(range(layers)):
        w_qkv, w_out, w_up, w_down = whole[layer]
        shift1, scale1, gate1, shift2, scale2, gate2 = [modulation[layer, k] for k in range(6)]
        (stream, attn_in, query, keys, values, mix, lse, attn_low, branch1, middle, mlp_in, up_proj, gelu_low, branch2) = saved[layer]
        d_gate2 = jnp.sum(upstream * branch2, axis=0)
        d_branch2 = (gate2 * upstream).astype(bf16)
        g_down = dot_first(gelu_low, d_branch2)
        d_gelu = dot_second(d_branch2, w_down)
        d_up = gelu_back(up_proj, d_gelu).astype(bf16)
        g_up = dot_first(mlp_in, d_up)
        d_mlp = dot_second(d_up, w_up)
        d_shift2 = jnp.sum(d_mlp, axis=0)
        d_scale2 = jnp.sum(d_mlp * layer_norm(middle), axis=0)
        d_mid = upstream + norm_back(middle, d_mlp * (1.0 + scale2))
        d_gate1 = jnp.sum(d_mid * branch1, axis=0)
        d_branch1 = (gate1 * d_mid).astype(bf16)
        g_out = dot_first(attn_low, d_branch1)
        d_attn = dot_second(d_branch1, w_out).astype(bf16)
        d_q, d_k, d_v = attend_back(query, keys, values, permit, mix, lse, heads_of(d_attn))
        pair = jnp.concatenate([rows_of(d_k), rows_of(d_v)], axis=1).astype(bf16)
        pair = scatter(pair.reshape(-1, count, 2 * width), near)
        d_qkv = jnp.concatenate([rows_of(d_q).astype(bf16), pair], axis=1)
        g_qkv = dot_first(attn_in, d_qkv)
        d_in = dot_second(d_qkv, w_qkv)
        d_shift1 = jnp.sum(d_in, axis=0)
        d_scale1 = jnp.sum(d_in * layer_norm(stream), axis=0)
        upstream = d_mid + norm_back(stream, d_in * (1.0 + scale1))
        mods[layer] = jnp.stack([d_shift1, d_scale1, d_gate1, d_shift2, d_scale2, d_gate2])
        grads[layer] = [
            scatter(pack(g.astype(bf16), order, s.shape[1], s.shape[2]), full).astype(f32)
            for g, s in zip((g_qkv, g_out, g_up, g_down), shards)
        ]
    patches_grad = band_rows(upstream.astype(bf16), bits)

    d_mod = jnp.stack(mods)
    for stage in near:
        d_mod = d_mod + swap(d_mod, stage)
    d_mod = gather(d_mod, bits.item)
    d_mod = d_mod.reshape(bits.items, layers, bits.batch, columns).transpose(2, 0, 1, 3)
    d_mod = jnp.take(d_mod, batch_at ^ jnp.arange(bits.batch, dtype=jnp.int32), axis=0)
    d_mod = spread(d_mod, bits.bs)
    d_mod = jnp.take(d_mod, mine ^ jnp.arange(bits.items, dtype=jnp.int32), axis=1)
    d_mod = d_mod.reshape(-1, layers, columns)
    ada_grad = jnp.stack(
        [lax.dot_general(cond.astype(f32), d_mod[:, layer], (((0,), (0,)), ((), ())), precision=highest) for layer in range(layers)]
    )
    d_cond = sum(
        lax.dot_general(d_mod[:, layer], ada[layer].astype(f32), (((1,), (1,)), ((), ())), precision=highest)
        for layer in range(layers)
    )
    d_embed = jax.vjp(jax.nn.silu, embed)[1](d_cond)[0]
    table_part = lax.dot_general(hot, d_embed, (((0,), (0,)), ((), ())), precision=highest)
    table_grad = scatter(table_part.reshape(bits.batch, table_rows, lat_cols), bits.bs)
    return (
        output,
        patches_grad,
        table_grad,
        ada_grad,
        jnp.stack([g[0] for g in grads]),
        jnp.stack([g[1] for g in grads]),
        jnp.stack([g[2] for g in grads]),
        jnp.stack([g[3] for g in grads]),
    )


def solution(mesh):
    batch, lat = mesh.shape["batch"], mesh.shape["lat"]

    def run(*arrays):
        bits = Bits(batch, lat, arrays[0].shape[0] // batch)
        rows = P("batch", "lat", None)
        weight = P(None, "lat", "batch")
        return jax.shard_map(
            lambda *pieces: per_device(bits, *pieces),
            mesh=mesh,
            in_specs=(rows, P("batch", "lat"), P("batch"), P("batch", "lat"), weight, weight, weight, weight, weight, rows),
            out_specs=(rows, rows, P("batch", "lat"), weight, weight, weight, weight, weight),
            check_vma=False,
        )(*arrays)

    return run
```

```python
import math
from functools import partial

import jax
import jax.numpy as jnp
from jax import lax
from jax.experimental import pallas as pl
from jax.experimental.pallas import tpu as pltpu
from jax.sharding import PartitionSpec as P

HEADS = 6
eps = 1e-06
masked_score = -1e30
needed_levels = 9
flag_rows = 16
highest = lax.Precision.HIGHEST
bf16 = jnp.bfloat16
f32 = jnp.float32


class Bits:
    def __init__(self, batch, lat, items):
        group = lat // items
        self.batch, self.lat, self.items, self.group = batch, lat, items, group
        self.core = ("lat", 1, lat)
        self.zs = [("lat", 1 << k, lat) for k in range(1, group.bit_length() - 1)]
        self.item = [("lat", group << k, lat) for k in range(items.bit_length() - 1)]
        self.bs = [("batch", 1 << k, batch) for k in range(batch.bit_length() - 1)]
        self.full = self.zs + self.item + self.bs + [self.core]


def swap(array, stage):
    name, mask, size = stage
    return lax.ppermute(array, name, [(i, i ^ mask) for i in range(size)])


def slot_masks(stages):
    masks = []
    for slot in range(1 << len(stages)):
        far = {"lat": 0, "batch": 0}
        for place, (name, mask, size) in enumerate(stages):
            if slot >> place & 1:
                far[name] |= mask
        masks.append((far["lat"], far["batch"]))
    return masks


def gather(array, stages):
    held = array[None]
    for stage in stages:
        held = jnp.concatenate([held, swap(held, stage)], axis=0)
    return held


def gather_parts(array, joined, apart):
    parts = [gather(array, joined)]
    for stage in apart:
        parts = parts + [swap(part, stage) for part in parts]
    return parts


def scatter(array, stages):
    for stage in reversed(stages):
        half = array.shape[0] // 2
        got = swap(array[half:], stage)
        array = (array[:half].astype(f32) + got.astype(f32)).astype(array.dtype)
    return array[0]


def spread(array, stages):
    held = array[:, None]
    for stage in reversed(stages):
        half = held.shape[0] // 2
        got = swap(held[half:], stage)
        held = jnp.stack([held[:half], got], axis=2)
        held = held.reshape((half, -1) + held.shape[3:])
    return held[0]


def call(body, outs, ins, scalars=None, scratch=(), name=None):
    specs = [pl.BlockSpec(memory_space=pltpu.VMEM)] * len(ins)
    args = list(ins)
    if scalars is not None:
        specs = [pl.BlockSpec(memory_space=pltpu.SMEM)] + specs
        args = [scalars] + args
    return pl.pallas_call(
        body,
        out_shape=[jax.ShapeDtypeStruct(shape, kind) for shape, kind in outs],
        in_specs=specs,
        out_specs=[pl.BlockSpec(memory_space=pltpu.VMEM)] * len(outs),
        scratch_shapes=list(scratch),
        name=name,
    )(*args)


def dot(left, right):
    return jnp.dot(left, right, preferred_element_type=f32)


def dot_rows(left, right):
    return lax.dot_general(left, right, (((0,), (0,)), ((), ())), preferred_element_type=f32)


def dot_cols(left, right):
    return lax.dot_general(left, right, (((1,), (1,)), ((), ())), preferred_element_type=f32)


def norm(values):
    center = values - jnp.mean(values, axis=-1, keepdims=True)
    inverse = lax.rsqrt(jnp.mean(center * center, axis=-1, keepdims=True) + eps)
    return center * inverse, inverse


def norm_back(normal, inverse, upstream):
    along = jnp.mean(upstream * normal, axis=-1, keepdims=True)
    return (upstream - jnp.mean(upstream, axis=-1, keepdims=True) - normal * along) * inverse


def total_rows(values):
    return jnp.sum(values, axis=0, keepdims=True)


gelu_scale = math.sqrt(2.0 / math.pi)


def gelu_parts(values):
    square = values * values
    bent = jnp.tanh(gelu_scale * (values + 0.044715 * values * square))
    return square, bent


def piece(mod, layer, index, width):
    return mod[layer : layer + 1, index * width : (index + 1) * width]


def pack_shards(shards, layer):
    qkv, out, up, down = [shard[layer] for shard in shards]
    rows = qkv.shape[0]
    blocks = down.shape[0] // rows
    first = jnp.concatenate([qkv, out], axis=1)
    low = jnp.concatenate([down[k * rows : (k + 1) * rows] for k in range(blocks)], axis=1)
    return first, jnp.concatenate([up, low], axis=0)


def pack_kernel(blocks, items, pos, qkv, out, up, down, patches, levels, cot, *outs):
    rows = qkv.shape[1]
    firsts, seconds, loads = outs[:2], outs[2:4], outs[4:]
    for layer in range(2):
        firsts[layer][...] = jnp.concatenate([qkv[layer], out[layer]], axis=1)
        seconds[layer][:rows] = up[layer]
        seconds[layer][rows:] = jnp.concatenate(
            [down[layer, k * rows : (k + 1) * rows] for k in range(blocks)], axis=1
        )
    load_kernel(items, pos, patches, levels, cot, *loads)


def load_kernel(items, pos, patches, levels, cot, *loads):
    rows, width = patches.shape[1:]
    for far in range(items):
        at = pos[2] ^ far
        load = loads[far]
        load[:rows] = patches[at]
        load[rows : 2 * rows] = cot[at]
        load[2 * rows :] = jnp.zeros((flag_rows, width), bf16)
        flags = (levels[pl.ds(at, 1), :] >= needed_levels).astype(f32).astype(bf16)
        load[2 * rows : 2 * rows + 1, :rows] = flags


def unpack_first_kernel(masks, share, columns, pos, *refs):
    parts, qkv, out, held = refs[:-3], refs[-3], refs[-2], refs[-1]
    rows = parts[0].shape[1]
    for slot, (lat_far, batch_far) in enumerate(masks):
        row = pl.multiple_of((pos[0] ^ lat_far) * rows, rows)
        held[pos[1] ^ batch_far, pl.ds(row, rows), :] = parts[slot // share][slot % share]
    batch = held.shape[0]
    qkv[...] = jnp.concatenate([held[b, :, :columns] for b in range(batch)], axis=1)
    out[...] = jnp.concatenate([held[b, :, columns:] for b in range(batch)], axis=1)


def unpack_second_kernel(masks, share, pos, *refs):
    parts, up, down, held = refs[:-3], refs[-3], refs[-2], refs[-1]
    rows = parts[0].shape[1] // 2
    for slot, (lat_far, batch_far) in enumerate(masks):
        row = pl.multiple_of((pos[0] ^ lat_far) * rows, rows)
        source = parts[slot // share]
        held[0, pos[1] ^ batch_far, pl.ds(row, rows), :] = source[slot % share, :rows]
        held[1, pos[1] ^ batch_far, pl.ds(row, rows), :] = source[slot % share, rows:]
    batch, height, units = held.shape[1:]
    up[...] = jnp.concatenate([held[0, b] for b in range(batch)], axis=1)
    thin = down.shape[1] // batch
    blocks = units // thin
    for k in range(blocks):
        block = jnp.concatenate([held[1, b, :, k * thin : (k + 1) * thin] for b in range(batch)], axis=1)
        for lat in range(height // rows):
            first = (lat * blocks + k) * rows
            down[first : first + rows] = block[lat * rows : (lat + 1) * rows]


def pack_first_kernel(masks, columns, pos, qkv, out, keep, send, held):
    batch, rows = held.shape[0], keep.shape[1]
    thin = held.shape[2] - columns
    for b in range(batch):
        held[b] = jnp.concatenate(
            [qkv[:, b * columns : (b + 1) * columns], out[:, b * thin : (b + 1) * thin]], axis=1
        )
    half = keep.shape[0]
    for slot, (lat_far, batch_far) in enumerate(masks):
        row = pl.multiple_of((pos[0] ^ lat_far) * rows, rows)
        target = keep if slot < half else send
        target[slot % half] = held[pos[1] ^ batch_far, pl.ds(row, rows), :]


def pack_second_kernel(masks, pos, up, down, keep, send, held):
    batch, height, units = held.shape[1:]
    rows = keep.shape[1] // 2
    thin = down.shape[1] // batch
    blocks = units // thin
    for b in range(batch):
        held[0, b] = up[:, b * units : (b + 1) * units]
        for lat in range(height // rows):
            firsts = [(lat * blocks + k) * rows for k in range(blocks)]
            held[1, b, lat * rows : (lat + 1) * rows] = jnp.concatenate(
                [down[first : first + rows, b * thin : (b + 1) * thin] for first in firsts], axis=1
            )
    half = keep.shape[0]
    for slot, (lat_far, batch_far) in enumerate(masks):
        row = pl.multiple_of((pos[0] ^ lat_far) * rows, rows)
        target = keep if slot < half else send
        target[slot % half, :rows] = held[0, pos[1] ^ batch_far, pl.ds(row, rows), :]
        target[slot % half, rows:] = held[1, pos[1] ^ batch_far, pl.ds(row, rows), :]


def add_kernel(held, got, *outs):
    half = held.shape[0] // len(outs)
    for place, out in enumerate(outs):
        rows = slice(place * half, (place + 1) * half)
        out[...] = (held[rows].astype(f32) + got[rows].astype(f32)).astype(out.dtype)


def slots_whole(parts, masks, pos):
    held = jnp.concatenate(parts, axis=0)
    return held


def order_of(bits, stages):
    lat_far = jnp.arange(bits.lat, dtype=jnp.int32) ^ lax.axis_index("lat")
    batch_far = jnp.arange(bits.batch, dtype=jnp.int32) ^ lax.axis_index("batch")
    slots = jnp.zeros((bits.lat, bits.batch), jnp.int32)
    for place, (name, mask, size) in enumerate(stages):
        far = lat_far[:, None] if name == "lat" else batch_far[None, :]
        slots = slots + jnp.where((far & mask) != 0, 1 << place, 0)
    return slots.reshape(-1)


def whole_of(held, order, bits):
    rows, columns = held.shape[1:]
    picked = jnp.take(held, order, axis=0).reshape(bits.lat, bits.batch, rows, columns)
    return picked.transpose(0, 2, 1, 3).reshape(bits.lat * rows, bits.batch * columns)


def slots_of(whole, order, bits):
    rows, columns = whole.shape[0] // bits.lat, whole.shape[1] // bits.batch
    split = whole.reshape(bits.lat, rows, bits.batch, columns).transpose(0, 2, 1, 3)
    return jnp.take(split.reshape(bits.lat * bits.batch, rows, columns), jnp.argsort(order), axis=0)


class Weights:
    def __init__(self, bits, shards, pos):
        self.bits, self.pos = bits, pos
        qkv, out, up, down = shards
        self.rows = qkv.shape[1]
        self.columns, self.thin = qkv.shape[2], out.shape[2]
        self.units = up.shape[2]
        self.width = self.rows * bits.lat
        self.hidden = down.shape[1] * bits.lat
        self.masks = slot_masks(bits.full)
        self.tiled = self.rows % 16 == 0 and self.units % 128 == 0
        self.joined = bits.zs + bits.item
        self.apart = bits.bs + [bits.core]
        self.share = 1 << len(self.joined)
        self.order = None if self.tiled else order_of(bits, bits.full)

    def first(self, shard):
        parts = gather_parts(shard, self.joined, self.apart)
        width, columns = self.width, self.columns
        if self.tiled:
            return call(
                partial(unpack_first_kernel, self.masks, self.share, columns),
                [((width, 3 * width), bf16), ((width, width), bf16)],
                parts,
                self.pos,
                [pltpu.VMEM((self.bits.batch, width, self.units), bf16)],
                name="unpack_first",
            )
        held = jnp.concatenate(parts, axis=0)
        return (
            whole_of(held[:, :, :columns], self.order, self.bits),
            whole_of(held[:, :, columns:], self.order, self.bits),
        )

    def second(self, shard):
        parts = gather_parts(shard, self.joined, self.apart)
        width, hidden, rows = self.width, self.hidden, self.rows
        if self.tiled:
            return call(
                partial(unpack_second_kernel, self.masks, self.share),
                [((width, hidden), bf16), ((hidden, width), bf16)],
                parts,
                self.pos,
                [pltpu.VMEM((2, self.bits.batch, width, self.units), bf16)],
                name="unpack_second",
            )
        held = jnp.concatenate(parts, axis=0)
        low = held[:, rows:]
        low = jnp.concatenate(
            [low[:, :, k * self.thin : (k + 1) * self.thin] for k in range(self.units // self.thin)], axis=1
        )
        return whole_of(held[:, :rows], self.order, self.bits), whole_of(low, self.order, self.bits)

    def first_sum(self, qkv, out):
        half = len(self.masks) // 2
        shape = (half, self.rows, self.units)
        if self.tiled:
            keep, send = call(
                partial(pack_first_kernel, self.masks, self.columns),
                [(shape, bf16), (shape, bf16)],
                [qkv, out],
                self.pos,
                [pltpu.VMEM((self.bits.batch, self.width, self.units), bf16)],
                name="pack_first",
            )
        else:
            held = jnp.concatenate(
                [slots_of(qkv, self.order, self.bits), slots_of(out, self.order, self.bits)], axis=2
            )
            keep, send = held[:half], held[half:]
        return self.sum(keep, send)

    def second_sum(self, up, down):
        half = len(self.masks) // 2
        shape = (half, 2 * self.rows, self.units)
        if self.tiled:
            keep, send = call(
                partial(pack_second_kernel, self.masks),
                [(shape, bf16), (shape, bf16)],
                [up, down],
                self.pos,
                [pltpu.VMEM((2, self.bits.batch, self.width, self.units), bf16)],
                name="pack_second",
            )
        else:
            low = slots_of(down, self.order, self.bits)
            rows = self.rows
            low = jnp.concatenate(
                [low[:, k * rows : (k + 1) * rows] for k in range(self.units // self.thin)], axis=2
            )
            held = jnp.concatenate([slots_of(up, self.order, self.bits), low], axis=1)
            keep, send = held[:half], held[half:]
        return self.sum(keep, send)

    def sum(self, keep, send):
        for stage in reversed(self.bits.full):
            got = swap(send, stage)
            shape = keep.shape
            if shape[0] == 1:
                return call(add_kernel, [(shape, f32)], [keep, got], name="add_last")[0][0]
            half = (shape[0] // 2,) + shape[1:]
            keep, send = call(add_kernel, [(half, bf16), (half, bf16)], [keep, got], name="add_halves")


def normed(values, shift, scale):
    return (norm(values)[0] * (1.0 + scale) + shift).astype(bf16)


def emit_qkv(rows, mod, layer, weight, attn_ref, query_ref, pair_ref, flags):
    width = rows.shape[1]
    attn_in = normed(rows, piece(mod, layer, 0, width), piece(mod, layer, 1, width))
    attn_ref[...] = attn_in
    query_ref[...] = dot(attn_in, weight[:, :width]).astype(bf16)
    count = rows.shape[0]
    pair_ref[0, :count] = dot(attn_in, weight[:, width:]).astype(bf16)
    pair_ref[0, count:] = flags


def start_kernel(items, mod, weight, *refs):
    loads = refs[:items]
    rows_ref, cot_ref, attn_ref, query_ref, pair_ref = refs[items:]
    count = (loads[0].shape[0] - flag_rows) // 2
    width = rows_ref.shape[1]
    rows = jnp.concatenate([load[:count] for load in loads], axis=0).astype(f32)
    rows_ref[...] = rows
    for far in range(items):
        cot_ref[far * count : (far + 1) * count] = loads[far][count : 2 * count].astype(f32)
    marks = [load[2 * count :, :count] for load in loads]
    rest = 2 * width - items * count
    flags = jnp.concatenate(marks + [jnp.zeros((flag_rows, rest), bf16)], axis=1)
    emit_qkv(rows, mod, 0, weight, attn_ref, query_ref, pair_ref, flags)


def split_heads(values):
    low = lax.broadcasted_iota(jnp.int32, values.shape, 1) < values.shape[1] // 2
    zero = jnp.zeros_like(values)
    return jnp.concatenate([jnp.where(low, values, zero), jnp.where(low, zero, values)], axis=0)


def join_heads(values):
    count = values.shape[0] // 2
    low = lax.broadcasted_iota(jnp.int32, (count, values.shape[1]), 1) < values.shape[1] // 2
    return jnp.where(low, values[:count], values[count:])


def pieces_of(refs):
    return [(ref, k) for ref in refs for k in range(ref.shape[0])]


def scores_of(queries, keys, flags, own):
    score = dot_cols(queries, keys)
    allow = flags.astype(f32) > 0.5
    if own:
        count = keys.shape[0]
        shape = score.shape
        query_at = lax.broadcasted_iota(jnp.int32, shape, 0)
        query_at = jnp.where(query_at >= count, query_at - count, query_at)
        allow = allow | (query_at == lax.broadcasted_iota(jnp.int32, shape, 1))
        return jnp.where(allow, score, masked_score)
    return score + jnp.where(allow, 0.0, masked_score)


def attend(query_ref, pair_refs, mix_ref, lse_ref):
    count, width = query_ref.shape
    pieces = pieces_of(pair_refs)
    scale = 1.0 / math.sqrt(width // HEADS)
    lane = lax.broadcasted_iota(jnp.int32, lse_ref.shape, 1)
    lse = jnp.zeros(lse_ref.shape, f32)
    for pair in range(HEADS // 2):
        at = slice(pair * 128, (pair + 1) * 128)
        past = slice(width + pair * 128, width + (pair + 1) * 128)
        queries = split_heads((query_ref[:, at].astype(f32) * scale).astype(bf16))
        scores = []
        for place, (ref, k) in enumerate(pieces):
            flags = ref[k, count : count + 1, :count]
            scores.append(scores_of(queries, ref[k, :count, at], flags, place == 0))
        top = jnp.max(scores[0], axis=-1, keepdims=True)
        for score in scores[1:]:
            top = jnp.maximum(top, jnp.max(score, axis=-1, keepdims=True))
        total, mixed = 0.0, 0.0
        for score, (ref, k) in zip(scores, pieces):
            grown = jnp.exp(score - top)
            total = total + jnp.sum(grown, axis=-1, keepdims=True)
            mixed = mixed + dot(grown.astype(bf16), ref[k, :count, past])
        mix_ref[:, at] = join_heads(mixed / total)
        logs = top + jnp.log(total)
        lse = jnp.where(lane == 2 * pair, logs[:count], lse)
        lse = jnp.where(lane == 2 * pair + 1, logs[count:], lse)
    lse_ref[...] = lse


def forward_rest(rows, mix, mod, layer, out, up, down):
    width = rows.shape[1]
    attn_low = mix.astype(bf16)
    branch1 = dot(attn_low, out[...])
    middle = rows + piece(mod, layer, 2, width) * branch1
    mlp_in = normed(middle, piece(mod, layer, 3, width), piece(mod, layer, 4, width))
    up_proj = dot(mlp_in, up[...])
    square, bent = gelu_parts(up_proj)
    gelu_low = (0.5 * up_proj * (1.0 + bent)).astype(bf16)
    branch2 = dot(gelu_low, down[...])
    result = middle + piece(mod, layer, 5, width) * branch2
    return attn_low, branch1, middle, mlp_in, up_proj, square, bent, gelu_low, branch2, result


def forward_kernel(layer, pairs, mod, rows, query, *refs):
    pair_refs, refs = refs[:pairs], refs[pairs:]
    out, up, down, qkv_next = refs[:4]
    mix, lse, branch1, middle, up_proj, branch2, stream, attn_next, query_next, pair_next = refs[4:]
    attend(query, pair_refs, mix, lse)
    kept = forward_rest(rows[...], mix[...], mod, layer, out, up, down)
    branch1[...], middle[...], up_proj[...], branch2[...] = kept[1], kept[2], kept[4], kept[8]
    stream[...] = kept[9]
    count = rows.shape[0]
    emit_qkv(kept[9], mod, layer + 1, qkv_next[...], attn_next, query_next, pair_next, pair_refs[0][0, count:])


def mlp_back(upstream, mod, layer, out, up, down, kept, d_mod, grads):
    attn_low, branch1, middle, mlp_in, up_proj, square, bent, gelu_low, branch2 = kept
    g_out, g_up, g_down, d_attn = grads
    width = upstream.shape[1]
    d_mod[2:3] = total_rows(upstream * branch2)
    d_branch2 = (piece(mod, layer, 5, width) * upstream).astype(bf16)
    g_down[...] = dot_rows(gelu_low, d_branch2).astype(bf16)
    d_gelu = dot_cols(d_branch2, down[...])
    slope = 0.5 * (1.0 + bent) + 0.5 * up_proj * (1.0 - bent * bent) * (
        gelu_scale * (1.0 + 3.0 * 0.044715 * square)
    )
    d_up = (d_gelu * slope).astype(bf16)
    g_up[...] = dot_rows(mlp_in, d_up).astype(bf16)
    d_mlp = dot_cols(d_up, up[...])
    normal, inverse = norm(middle)
    d_mod[0:1] = total_rows(d_mlp)
    d_mod[1:2] = total_rows(d_mlp * normal)
    d_mid = upstream + norm_back(normal, inverse, d_mlp * (1.0 + piece(mod, layer, 4, width)))
    d_mod[3:4] = total_rows(d_mid * branch1)
    d_mod[4:8] = jnp.zeros((4, width), f32)
    d_branch1 = (piece(mod, layer, 2, width) * d_mid).astype(bf16)
    g_out[...] = dot_rows(attn_low, d_branch1).astype(bf16)
    d_attn[...] = dot_cols(d_branch1, out[...]).astype(bf16)
    return d_mid


def turn_kernel(layer, pairs, mod, rows, query, *refs):
    pair_refs, refs = refs[:pairs], refs[pairs:]
    out, up, down, cot = refs[:4]
    mix, lse, output, d_mid, d_mod, g_out, g_up, g_down, d_attn = refs[4:]
    attend(query, pair_refs, mix, lse)
    kept = forward_rest(rows[...], mix[...], mod, layer, out, up, down)
    output[...] = kept[9].astype(bf16)
    d_mid[...] = mlp_back(cot[...], mod, layer, out, up, down, kept[:9], d_mod, (g_out, g_up, g_down, d_attn))


def attend_back_kernel(pairs, query_ref, mix_ref, lse_ref, grad_ref, *refs):
    pair_refs, d_query, d_pairs = refs[:pairs], refs[pairs], refs[pairs + 1 :]
    count, width = query_ref.shape
    pieces, d_pieces = pieces_of(pair_refs), pieces_of(d_pairs)
    scale = 1.0 / math.sqrt(width // HEADS)
    for pair in range(HEADS // 2):
        at = slice(pair * 128, (pair + 1) * 128)
        past = slice(width + pair * 128, width + (pair + 1) * 128)
        queries = split_heads((query_ref[:, at].astype(f32) * scale).astype(bf16))
        grad = grad_ref[:, at]
        grads = split_heads(grad)
        delta = jnp.sum(split_heads(grad.astype(f32) * mix_ref[:, at]), axis=-1, keepdims=True)
        logs = jnp.concatenate(
            [lse_ref[:, 2 * pair : 2 * pair + 1], lse_ref[:, 2 * pair + 1 : 2 * pair + 2]], axis=0
        )
        d_q = 0.0
        for place, ((ref, k), (d_ref, d_k)) in enumerate(zip(pieces, d_pieces)):
            keys, values = ref[k, :count, at], ref[k, :count, past]
            flags = ref[k, count : count + 1, :count]
            prob = jnp.exp(scores_of(queries, keys, flags, place == 0) - logs)
            d_prob = dot_cols(grads, values)
            d_score = (prob * (d_prob - delta)).astype(bf16)
            d_ref[d_k, :, past] = dot_rows(prob.astype(bf16), grads).astype(bf16)
            d_ref[d_k, :, at] = dot_rows(d_score, queries).astype(bf16)
            d_q = d_q + dot(d_score, keys)
        d_query[:, at] = (join_heads(d_q) * scale).astype(bf16)


def qkv_back(d_query, d_parts, attn_in, rows, mod, layer, weight, d_mid, g_qkv, d_mod):
    width = rows.shape[1]
    d_pair = d_parts[0][0].astype(f32)
    for part in d_parts[1:]:
        d_pair = d_pair + part[0].astype(f32)
    d_pair = d_pair.astype(bf16)
    g_qkv[:, :width] = dot_rows(attn_in[...], d_query[...]).astype(bf16)
    g_qkv[:, width:] = dot_rows(attn_in[...], d_pair).astype(bf16)
    d_in = dot_cols(d_query[...], weight[:, :width]) + dot_cols(d_pair, weight[:, width:])
    normal, inverse = norm(rows[...])
    d_mod[0:1] = total_rows(d_in)
    d_mod[1:2] = total_rows(d_in * normal)
    d_mod[2:8] = jnp.zeros((6, width), f32)
    return d_mid[...] + norm_back(normal, inverse, d_in * (1.0 + piece(mod, layer, 1, width)))


def qkv_back_kernel(layer, count, mod, d_query, *refs):
    parts, refs = refs[:count], refs[count:]
    attn_in, rows, weight, d_mid, upstream, g_qkv, d_mod = refs
    upstream[...] = qkv_back(
        d_query, parts, attn_in, rows, mod, layer, weight, d_mid, g_qkv, d_mod
    ).astype(upstream.dtype)


def mlp_back_kernel(layer, mod, upstream, mix, branch1, middle, up_proj, branch2, out, up, down, *refs):
    d_mid, d_mod = refs[:2]
    width = upstream.shape[1]
    mlp_in = normed(middle[...], piece(mod, layer, 3, width), piece(mod, layer, 4, width))
    square, bent = gelu_parts(up_proj[...])
    gelu_low = (0.5 * up_proj[...] * (1.0 + bent)).astype(bf16)
    kept = (mix[...].astype(bf16), branch1[...], middle[...], mlp_in, up_proj[...], square, bent, gelu_low, branch2[...])
    d_mid[...] = mlp_back(upstream[...], mod, layer, out, up, down, kept, d_mod, refs[2:])


def band_rows(array, bits):
    mine = lax.axis_index("lat") // bits.group
    rows = array.shape[0] // bits.items
    parts = []
    for far in range(bits.items):
        part = array[far * rows : (far + 1) * rows]
        if far:
            part = swap(part, ("lat", far * bits.group, bits.lat))
        parts.append(part)
    stacked = jnp.stack(parts)
    order = jnp.arange(bits.items, dtype=jnp.int32) ^ mine
    return jnp.take(stacked, order, axis=0)


def per_device(bits, patches, levels, lead_index, lead_table, ada, qkv, out, up, down, cotangent):
    layers = qkv.shape[0]
    band, width = patches.shape[1:]
    count = band * bits.items
    lat_at, batch_at = lax.axis_index("lat"), lax.axis_index("batch")
    mine = lat_at // bits.group
    pos = jnp.stack([lat_at, batch_at, mine]).astype(jnp.int32)
    shards = (qkv, out, up, down)
    weights = Weights(bits, shards, pos)

    load_shape = ((2 * band + flag_rows, width), bf16)
    if weights.tiled:
        rows, units = weights.rows, weights.units
        packed = call(
            partial(pack_kernel, down.shape[1] // rows, bits.items),
            [((rows, units), bf16)] * 2 + [((2 * rows, units), bf16)] * 2 + [load_shape] * bits.items,
            [qkv, out, up, down, patches, levels, cotangent],
            pos,
            name="pack",
        )
        firsts, seconds, loads = packed[:2], packed[2:4], packed[4:]
    else:
        both = [pack_shards(shards, layer) for layer in range(layers)]
        firsts, seconds = [pair[0] for pair in both], [pair[1] for pair in both]
        loads = call(partial(load_kernel, bits.items), [load_shape] * bits.items, [patches, levels, cotangent], pos)
    loads = [loads[0]] + [
        swap(loads[far], ("lat", far * bits.group, bits.lat)) for far in range(1, bits.items)
    ]

    table_rows, lat_cols = lead_table.shape
    lead_row = jnp.broadcast_to(lead_index.astype(f32)[None], (table_rows, bits.items))
    lead_row = jnp.concatenate([lead_table.astype(f32), lead_row], axis=1)
    got = gather(lead_row, bits.bs)
    batch_far = jnp.arange(bits.batch, dtype=jnp.int32)
    row_ids = ((batch_at ^ batch_far)[:, None] * table_rows + jnp.arange(table_rows)[None]).reshape(-1)
    table = got[:, :, :lat_cols].reshape(-1, lat_cols)
    leads = got[:, 0, lat_cols:].reshape(-1)
    hot = (leads[:, None] == row_ids[None, :].astype(f32)).astype(f32)
    embed = jnp.dot(hot, table, precision=highest)
    cond = jax.nn.silu(embed).astype(bf16)
    part = jnp.stack([dot(cond, ada[layer]) for layer in range(layers)], axis=1)
    columns = part.shape[-1]
    part = part.reshape(bits.batch, bits.items, layers, columns)
    part = jnp.take(part, mine ^ jnp.arange(bits.items, dtype=jnp.int32), axis=1)
    part = part.transpose(1, 0, 2, 3)
    part = scatter(part, bits.item)
    for stage in bits.zs + [bits.core]:
        part = part + swap(part, stage)
    part = spread(part, bits.bs)
    part = jnp.take(part, batch_at ^ batch_far, axis=0)
    mod = part.transpose(1, 0, 2).reshape(layers, 6 * width)

    whole = [weights.first(firsts[0]) + weights.second(seconds[0])]
    whole += [weights.first(firsts[layer]) + weights.second(seconds[layer]) for layer in range(1, layers)]

    rows_kind, low_kind = ((count, width), f32), ((count, width), bf16)
    pair_kind = ((1, count + flag_rows, 2 * width), bf16)
    lse_kind, mod_kind = ((count, 128), f32), ((8, width), f32)
    stream, cot, attn_in, query, pair = call(
        partial(start_kernel, bits.items),
        [rows_kind, rows_kind, low_kind, low_kind, pair_kind],
        [mod, whole[0][0]] + list(loads),
        name="start",
    )
    saved = []
    for layer in range(layers):
        w_qkv, w_out, w_up, w_down = whole[layer]
        chip = [pair]
        for stage in bits.zs:
            joined = chip[0] if len(chip) == 1 else jnp.concatenate(chip, axis=0)
            chip = chip + [swap(joined, stage)]
        pairs = chip + [swap(part, bits.core) for part in chip]
        given = [mod, stream, query] + pairs + [w_out, w_up, w_down]
        if layer + 1 < layers:
            wide = ((count, w_up.shape[1]), f32)
            mix, lse, branch1, middle, up_proj, branch2, result, attn_next, query_next, pair = call(
                partial(forward_kernel, layer, len(pairs)),
                [rows_kind, lse_kind, rows_kind, rows_kind, wide, rows_kind, rows_kind, low_kind, low_kind, pair_kind],
                given + [whole[layer + 1][0]],
                name="forward",
            )
            saved.append((stream, attn_in, query, pairs, mix, lse, branch1, middle, up_proj, branch2))
            stream, attn_in, query = result, attn_next, query_next
    square_kind = ((width, width), bf16)
    grad_kinds = [square_kind, (w_up.shape, bf16), (w_down.shape, bf16), low_kind]
    mix, lse, output, d_mid, d_mlp_mod, g_out, g_up, g_down, d_attn = call(
        partial(turn_kernel, layers - 1, len(pairs)),
        [rows_kind, lse_kind, low_kind, rows_kind, mod_kind] + grad_kinds,
        given + [cot],
        name="turn",
    )
    saved.append((stream, attn_in, query, pairs, mix, lse))
    output = band_rows(output, bits)

    grads, mods = [None] * layers, [None] * layers
    for layer in reversed(range(layers)):
        stream, attn_in, query, pairs, mix, lse = saved[layer][:6]
        second = weights.second_sum(g_up, g_down)
        backs = call(
            partial(attend_back_kernel, len(pairs)),
            [low_kind] + [((p.shape[0], count, 2 * width), bf16) for p in pairs],
            [query, mix, lse, d_attn] + pairs,
            name="attend_back",
        )
        d_query, d_chip, d_core = backs[0], backs[1 : 1 + len(pairs) // 2], backs[1 + len(pairs) // 2 :]
        got = [swap(part, bits.core) for part in d_core]
        parts = [d_chip[0], got[0]]
        if bits.zs:
            rest = [
                call(add_kernel, [(p.shape, bf16)], [p, q], name="add_pairs")[0]
                for p, q in zip(d_chip[1:], got[1:])
            ]
            held = [rest[0]] if len(rest) == 1 else rest
            for place in reversed(range(len(bits.zs))):
                back = swap(held[place], bits.zs[place])
                if place == 0:
                    parts.append(back)
                else:
                    parts.append(back[:1])
                    at = 1
                    for near in range(place):
                        size = held[near].shape[0]
                        held[near] = held[near] + back[at : at + size]
                        at += size
        upstream, g_qkv, d_qkv_mod = call(
            partial(qkv_back_kernel, layer, len(parts)),
            [rows_kind if layer else low_kind, ((width, 3 * width), bf16), mod_kind],
            [mod, d_query] + parts + [attn_in, stream, whole[layer][0], d_mid],
            name="qkv_back",
        )
        mods[layer] = jnp.concatenate([d_qkv_mod[0:2], d_mlp_mod[3:4], d_mlp_mod[0:3]], axis=0)
        grads[layer] = (weights.first_sum(g_qkv, g_out), second)
        if layer:
            w_out, w_up, w_down = whole[layer - 1][1:]
            mix, lse, branch1, middle, up_proj, branch2 = saved[layer - 1][4:]
            d_mid, d_mlp_mod, g_out, g_up, g_down, d_attn = call(
                partial(mlp_back_kernel, layer - 1),
                [rows_kind, mod_kind] + grad_kinds,
                [mod, upstream, mix, branch1, middle, up_proj, branch2, w_out, w_up, w_down],
                name="mlp_back",
            )
    patches_grad = band_rows(upstream, bits)

    d_mod = jnp.stack(mods)
    for stage in bits.zs + [bits.core]:
        d_mod = d_mod + swap(d_mod, stage)
    d_mod = gather(d_mod, bits.item)
    d_mod = d_mod.reshape(bits.items, layers, bits.batch, columns).transpose(2, 0, 1, 3)
    d_mod = jnp.take(d_mod, batch_at ^ batch_far, axis=0)
    d_mod = spread(d_mod, bits.bs)
    d_mod = jnp.take(d_mod, mine ^ jnp.arange(bits.items, dtype=jnp.int32), axis=1)
    d_mod = d_mod.reshape(-1, layers, columns)
    ada_grad = jnp.stack(
        [
            lax.dot_general(cond.astype(f32), d_mod[:, layer], (((0,), (0,)), ((), ())), precision=highest)
            for layer in range(layers)
        ]
    )
    d_cond = sum(
        lax.dot_general(d_mod[:, layer], ada[layer].astype(f32), (((1,), (1,)), ((), ())), precision=highest)
        for layer in range(layers)
    )
    d_embed = jax.vjp(jax.nn.silu, embed)[1](d_cond)[0]
    table_part = lax.dot_general(hot, d_embed, (((0,), (0,)), ((), ())), precision=highest)
    table_grad = scatter(table_part.reshape(bits.batch, table_rows, lat_cols), bits.bs)

    rows, cols, thin = weights.rows, weights.columns, weights.thin
    lows = [
        jnp.concatenate([pair[1][rows:, k * thin : (k + 1) * thin] for k in range(weights.units // thin)], axis=0)
        for pair in grads
    ]
    return (
        output,
        patches_grad,
        table_grad,
        ada_grad,
        jnp.stack([pair[0][:, :cols] for pair in grads]),
        jnp.stack([pair[0][:, cols:] for pair in grads]),
        jnp.stack([pair[1][:rows] for pair in grads]),
        jnp.stack(lows),
    )


def solution(mesh):
    batch, lat = mesh.shape["batch"], mesh.shape["lat"]

    def run(*arrays):
        bits = Bits(batch, lat, arrays[0].shape[0] // batch)
        rows = P("batch", "lat", None)
        weight = P(None, "lat", "batch")
        return jax.shard_map(
            lambda *pieces: per_device(bits, *pieces),
            mesh=mesh,
            in_specs=(rows, P("batch", "lat"), P("batch"), P("batch", "lat"), weight, weight, weight, weight, weight, rows),
            out_specs=(rows, rows, P("batch", "lat"), weight, weight, weight, weight, weight),
            check_vma=False,
        )(*arrays)

    return run
```

```python
import math
from functools import partial

import jax
import jax.numpy as jnp
from jax import lax
from jax.experimental import pallas as pl
from jax.experimental.pallas import tpu as pltpu
from jax.sharding import PartitionSpec as P

HEADS = 6
eps = 1e-06
masked_score = -1e30
needed_levels = 9
flag_rows = 16
highest = lax.Precision.HIGHEST
bf16 = jnp.bfloat16
f32 = jnp.float32


class Bits:
    def __init__(self, batch, lat, items):
        group = lat // items
        self.batch, self.lat, self.items, self.group = batch, lat, items, group
        self.core = ("lat", 1, lat)
        self.zs = [("lat", 1 << k, lat) for k in range(1, group.bit_length() - 1)]
        self.item = [("lat", group << k, lat) for k in range(items.bit_length() - 1)]
        self.bs = [("batch", 1 << k, batch) for k in range(batch.bit_length() - 1)]
        self.full = self.zs + self.item + self.bs + [self.core]


def swap(array, stage):
    name, mask, size = stage
    return lax.ppermute(array, name, [(i, i ^ mask) for i in range(size)])


def slot_masks(stages):
    masks = []
    for slot in range(1 << len(stages)):
        far = {"lat": 0, "batch": 0}
        for place, (name, mask, size) in enumerate(stages):
            if slot >> place & 1:
                far[name] |= mask
        masks.append((far["lat"], far["batch"]))
    return masks


def gather(array, stages):
    held = array[None]
    for stage in stages:
        held = jnp.concatenate([held, swap(held, stage)], axis=0)
    return held


def gather_parts(array, joined, apart):
    parts = [gather(array, joined)]
    for stage in apart:
        parts = parts + [swap(part, stage) for part in parts]
    return parts


def scatter(array, stages):
    for stage in reversed(stages):
        half = array.shape[0] // 2
        got = swap(array[half:], stage)
        array = (array[:half].astype(f32) + got.astype(f32)).astype(array.dtype)
    return array[0]


def spread(array, stages):
    held = array[:, None]
    for stage in reversed(stages):
        half = held.shape[0] // 2
        got = swap(held[half:], stage)
        held = jnp.stack([held[:half], got], axis=2)
        held = held.reshape((half, -1) + held.shape[3:])
    return held[0]


class Place:
    near = True


def call(body, outs, ins, scalars=None, scratch=(), name=None, limit=24):
    near = Place.near
    specs = [pl.BlockSpec(memory_space=pltpu.VMEM)] * len(ins)
    args = [pltpu.with_memory_space_constraint(x, pltpu.VMEM) for x in ins] if near else list(ins)
    if scalars is not None:
        specs = [pl.BlockSpec(memory_space=pltpu.SMEM)] + specs
        args = [scalars] + args
    kind = pltpu.VMEM if near else jax.ShapeDtypeStruct
    return pl.pallas_call(
        body,
        out_shape=[kind(shape, dtype) for shape, dtype in outs],
        in_specs=specs,
        out_specs=[pl.BlockSpec(memory_space=pltpu.VMEM)] * len(outs),
        scratch_shapes=list(scratch),
        compiler_params=pltpu.CompilerParams(vmem_limit_bytes=limit << 20) if near else None,
        name=name,
    )(*args)


def dot(left, right):
    return jnp.dot(left, right, preferred_element_type=f32)


def dot_rows(left, right):
    return lax.dot_general(left, right, (((0,), (0,)), ((), ())), preferred_element_type=f32)


def dot_cols(left, right):
    return lax.dot_general(left, right, (((1,), (1,)), ((), ())), preferred_element_type=f32)


def norm(values):
    center = values - jnp.mean(values, axis=-1, keepdims=True)
    inverse = lax.rsqrt(jnp.mean(center * center, axis=-1, keepdims=True) + eps)
    return center * inverse, inverse


def norm_back(normal, inverse, upstream):
    along = jnp.mean(upstream * normal, axis=-1, keepdims=True)
    return (upstream - jnp.mean(upstream, axis=-1, keepdims=True) - normal * along) * inverse


def total_rows(values):
    return jnp.sum(values, axis=0, keepdims=True)


gelu_scale = math.sqrt(2.0 / math.pi)


def gelu_parts(values):
    square = values * values
    bent = jnp.tanh(gelu_scale * (values + 0.044715 * values * square))
    return square, bent


def piece(mod, layer, index, width):
    return mod[layer : layer + 1, index * width : (index + 1) * width]


def pack_shards(shards, layer):
    qkv, out, up, down = [shard[layer] for shard in shards]
    rows = qkv.shape[0]
    blocks = down.shape[0] // rows
    first = jnp.concatenate([qkv, out], axis=1)
    low = jnp.concatenate([down[k * rows : (k + 1) * rows] for k in range(blocks)], axis=1)
    return first, jnp.concatenate([up, low], axis=0)


def pack_kernel(blocks, items, pos, qkv, out, up, down, patches, levels, cot, *outs):
    rows = qkv.shape[1]
    firsts, seconds, loads = outs[:2], outs[2:4], outs[4:]
    for layer in range(2):
        firsts[layer][...] = jnp.concatenate([qkv[layer], out[layer]], axis=1)
        seconds[layer][:rows] = up[layer]
        seconds[layer][rows:] = jnp.concatenate(
            [down[layer, k * rows : (k + 1) * rows] for k in range(blocks)], axis=1
        )
    load_kernel(items, pos, patches, levels, cot, *loads)


def load_kernel(items, pos, patches, levels, cot, *loads):
    rows, width = patches.shape[1:]
    for far in range(items):
        at = pos[2] ^ far
        load = loads[far]
        load[:rows] = patches[at]
        load[rows : 2 * rows] = cot[at]
        load[2 * rows :] = jnp.zeros((flag_rows, width), bf16)
        flags = (levels[pl.ds(at, 1), :] >= needed_levels).astype(f32).astype(bf16)
        load[2 * rows : 2 * rows + 1, :rows] = flags


def unpack_first_kernel(masks, share, columns, pos, *refs):
    parts, qkv, out, held = refs[:-3], refs[-3], refs[-2], refs[-1]
    rows = parts[0].shape[1]
    for slot, (lat_far, batch_far) in enumerate(masks):
        row = pl.multiple_of((pos[0] ^ lat_far) * rows, rows)
        held[pos[1] ^ batch_far, pl.ds(row, rows), :] = parts[slot // share][slot % share]
    batch = held.shape[0]
    qkv[...] = jnp.concatenate([held[b, :, :columns] for b in range(batch)], axis=1)
    out[...] = jnp.concatenate([held[b, :, columns:] for b in range(batch)], axis=1)


def unpack_second_kernel(masks, share, pos, *refs):
    parts, up, down, held = refs[:-3], refs[-3], refs[-2], refs[-1]
    rows = parts[0].shape[1] // 2
    for slot, (lat_far, batch_far) in enumerate(masks):
        row = pl.multiple_of((pos[0] ^ lat_far) * rows, rows)
        source = parts[slot // share]
        held[0, pos[1] ^ batch_far, pl.ds(row, rows), :] = source[slot % share, :rows]
        held[1, pos[1] ^ batch_far, pl.ds(row, rows), :] = source[slot % share, rows:]
    batch, height, units = held.shape[1:]
    up[...] = jnp.concatenate([held[0, b] for b in range(batch)], axis=1)
    thin = down.shape[1] // batch
    blocks = units // thin
    for k in range(blocks):
        block = jnp.concatenate([held[1, b, :, k * thin : (k + 1) * thin] for b in range(batch)], axis=1)
        for lat in range(height // rows):
            first = (lat * blocks + k) * rows
            down[first : first + rows] = block[lat * rows : (lat + 1) * rows]


def pack_first_kernel(masks, columns, pos, qkv, out, keep, send, held):
    batch, rows = held.shape[0], keep.shape[1]
    thin = held.shape[2] - columns
    for b in range(batch):
        held[b] = jnp.concatenate(
            [qkv[:, b * columns : (b + 1) * columns], out[:, b * thin : (b + 1) * thin]], axis=1
        )
    half = keep.shape[0]
    for slot, (lat_far, batch_far) in enumerate(masks):
        row = pl.multiple_of((pos[0] ^ lat_far) * rows, rows)
        target = keep if slot < half else send
        target[slot % half] = held[pos[1] ^ batch_far, pl.ds(row, rows), :]


def pack_second_kernel(masks, pos, up, down, keep, send, held):
    batch, height, units = held.shape[1:]
    rows = keep.shape[1] // 2
    thin = down.shape[1] // batch
    blocks = units // thin
    for b in range(batch):
        held[0, b] = up[:, b * units : (b + 1) * units]
        for lat in range(height // rows):
            firsts = [(lat * blocks + k) * rows for k in range(blocks)]
            held[1, b, lat * rows : (lat + 1) * rows] = jnp.concatenate(
                [down[first : first + rows, b * thin : (b + 1) * thin] for first in firsts], axis=1
            )
    half = keep.shape[0]
    for slot, (lat_far, batch_far) in enumerate(masks):
        row = pl.multiple_of((pos[0] ^ lat_far) * rows, rows)
        target = keep if slot < half else send
        target[slot % half, :rows] = held[0, pos[1] ^ batch_far, pl.ds(row, rows), :]
        target[slot % half, rows:] = held[1, pos[1] ^ batch_far, pl.ds(row, rows), :]


def add_kernel(held, got, *outs):
    half = held.shape[0] // len(outs)
    for place, out in enumerate(outs):
        rows = slice(place * half, (place + 1) * half)
        out[...] = (held[rows].astype(f32) + got[rows].astype(f32)).astype(out.dtype)


def slots_whole(parts, masks, pos):
    held = jnp.concatenate(parts, axis=0)
    return held


def order_of(bits, stages):
    lat_far = jnp.arange(bits.lat, dtype=jnp.int32) ^ lax.axis_index("lat")
    batch_far = jnp.arange(bits.batch, dtype=jnp.int32) ^ lax.axis_index("batch")
    slots = jnp.zeros((bits.lat, bits.batch), jnp.int32)
    for place, (name, mask, size) in enumerate(stages):
        far = lat_far[:, None] if name == "lat" else batch_far[None, :]
        slots = slots + jnp.where((far & mask) != 0, 1 << place, 0)
    return slots.reshape(-1)


def whole_of(held, order, bits):
    rows, columns = held.shape[1:]
    picked = jnp.take(held, order, axis=0).reshape(bits.lat, bits.batch, rows, columns)
    return picked.transpose(0, 2, 1, 3).reshape(bits.lat * rows, bits.batch * columns)


def slots_of(whole, order, bits):
    rows, columns = whole.shape[0] // bits.lat, whole.shape[1] // bits.batch
    split = whole.reshape(bits.lat, rows, bits.batch, columns).transpose(0, 2, 1, 3)
    return jnp.take(split.reshape(bits.lat * bits.batch, rows, columns), jnp.argsort(order), axis=0)


class Weights:
    def __init__(self, bits, shards, pos):
        self.bits, self.pos = bits, pos
        qkv, out, up, down = shards
        self.rows = qkv.shape[1]
        self.columns, self.thin = qkv.shape[2], out.shape[2]
        self.units = up.shape[2]
        self.width = self.rows * bits.lat
        self.hidden = down.shape[1] * bits.lat
        self.masks = slot_masks(bits.full)
        self.tiled = self.rows % 16 == 0 and self.units % 128 == 0
        self.joined = bits.zs + bits.item
        self.apart = bits.bs + [bits.core]
        self.share = 1 << len(self.joined)
        self.order = None if self.tiled else order_of(bits, bits.full)

    def first(self, shard):
        parts = gather_parts(shard, self.joined, self.apart)
        width, columns = self.width, self.columns
        if self.tiled:
            return call(
                partial(unpack_first_kernel, self.masks, self.share, columns),
                [((width, 3 * width), bf16), ((width, width), bf16)],
                parts,
                self.pos,
                [pltpu.VMEM((self.bits.batch, width, self.units), bf16)],
                name="unpack_first",
            )
        held = jnp.concatenate(parts, axis=0)
        return (
            whole_of(held[:, :, :columns], self.order, self.bits),
            whole_of(held[:, :, columns:], self.order, self.bits),
        )

    def second(self, shard):
        parts = gather_parts(shard, self.joined, self.apart)
        width, hidden, rows = self.width, self.hidden, self.rows
        if self.tiled:
            return call(
                partial(unpack_second_kernel, self.masks, self.share),
                [((width, hidden), bf16), ((hidden, width), bf16)],
                parts,
                self.pos,
                [pltpu.VMEM((2, self.bits.batch, width, self.units), bf16)],
                name="unpack_second",
            )
        held = jnp.concatenate(parts, axis=0)
        low = held[:, rows:]
        low = jnp.concatenate(
            [low[:, :, k * self.thin : (k + 1) * self.thin] for k in range(self.units // self.thin)], axis=1
        )
        return whole_of(held[:, :rows], self.order, self.bits), whole_of(low, self.order, self.bits)

    def first_sum(self, qkv, out):
        half = len(self.masks) // 2
        shape = (half, self.rows, self.units)
        if self.tiled:
            keep, send = call(
                partial(pack_first_kernel, self.masks, self.columns),
                [(shape, bf16), (shape, bf16)],
                [qkv, out],
                self.pos,
                [pltpu.VMEM((self.bits.batch, self.width, self.units), bf16)],
                name="pack_first",
            )
        else:
            held = jnp.concatenate(
                [slots_of(qkv, self.order, self.bits), slots_of(out, self.order, self.bits)], axis=2
            )
            keep, send = held[:half], held[half:]
        return self.sum(keep, send)

    def second_sum(self, up, down):
        half = len(self.masks) // 2
        shape = (half, 2 * self.rows, self.units)
        if self.tiled:
            keep, send = call(
                partial(pack_second_kernel, self.masks),
                [(shape, bf16), (shape, bf16)],
                [up, down],
                self.pos,
                [pltpu.VMEM((2, self.bits.batch, self.width, self.units), bf16)],
                name="pack_second",
            )
        else:
            low = slots_of(down, self.order, self.bits)
            rows = self.rows
            low = jnp.concatenate(
                [low[:, k * rows : (k + 1) * rows] for k in range(self.units // self.thin)], axis=2
            )
            held = jnp.concatenate([slots_of(up, self.order, self.bits), low], axis=1)
            keep, send = held[:half], held[half:]
        return self.sum(keep, send)

    def sum(self, keep, send):
        for stage in reversed(self.bits.full):
            got = swap(send, stage)
            shape = keep.shape
            if shape[0] == 1:
                return call(add_kernel, [(shape, f32)], [keep, got], name="add_last")[0][0]
            half = (shape[0] // 2,) + shape[1:]
            keep, send = call(add_kernel, [(half, bf16), (half, bf16)], [keep, got], name="add_halves")


def normed(values, shift, scale):
    return (norm(values)[0] * (1.0 + scale) + shift).astype(bf16)


def emit_qkv(rows, mod, layer, weight, attn_ref, query_ref, pair_ref, flags):
    width = rows.shape[1]
    attn_in = normed(rows, piece(mod, layer, 0, width), piece(mod, layer, 1, width))
    attn_ref[...] = attn_in
    query_ref[...] = dot(attn_in, weight[:, :width]).astype(bf16)
    count = rows.shape[0]
    pair_ref[0, :count] = dot(attn_in, weight[:, width:]).astype(bf16)
    pair_ref[0, count:] = flags


def start_kernel(items, mod, weight, *refs):
    loads = refs[:items]
    rows_ref, cot_ref, attn_ref, query_ref, pair_ref = refs[items:]
    count = (loads[0].shape[0] - flag_rows) // 2
    width = rows_ref.shape[1]
    rows = jnp.concatenate([load[:count] for load in loads], axis=0).astype(f32)
    rows_ref[...] = rows
    for far in range(items):
        cot_ref[far * count : (far + 1) * count] = loads[far][count : 2 * count].astype(f32)
    marks = [load[2 * count :, :count] for load in loads]
    rest = 2 * width - items * count
    flags = jnp.concatenate(marks + [jnp.zeros((flag_rows, rest), bf16)], axis=1)
    emit_qkv(rows, mod, 0, weight, attn_ref, query_ref, pair_ref, flags)


def split_heads(values):
    low = lax.broadcasted_iota(jnp.int32, values.shape, 1) < values.shape[1] // 2
    zero = jnp.zeros_like(values)
    return jnp.concatenate([jnp.where(low, values, zero), jnp.where(low, zero, values)], axis=0)


def join_heads(values):
    count = values.shape[0] // 2
    low = lax.broadcasted_iota(jnp.int32, (count, values.shape[1]), 1) < values.shape[1] // 2
    return jnp.where(low, values[:count], values[count:])


def pieces_of(refs):
    return [(ref, k) for ref in refs for k in range(ref.shape[0])]


def scores_of(queries, keys, flags, own):
    score = dot_cols(queries, keys)
    allow = flags.astype(f32) > 0.5
    if own:
        count = keys.shape[0]
        shape = score.shape
        query_at = lax.broadcasted_iota(jnp.int32, shape, 0)
        query_at = jnp.where(query_at >= count, query_at - count, query_at)
        allow = allow | (query_at == lax.broadcasted_iota(jnp.int32, shape, 1))
        return jnp.where(allow, score, masked_score)
    return score + jnp.where(allow, 0.0, masked_score)


def attend(query_ref, pair_refs, mix_ref, lse_ref):
    count, width = query_ref.shape
    pieces = pieces_of(pair_refs)
    scale = 1.0 / math.sqrt(width // HEADS)
    lane = lax.broadcasted_iota(jnp.int32, lse_ref.shape, 1)
    lse = jnp.zeros(lse_ref.shape, f32)
    for pair in range(HEADS // 2):
        at = slice(pair * 128, (pair + 1) * 128)
        past = slice(width + pair * 128, width + (pair + 1) * 128)
        queries = split_heads((query_ref[:, at].astype(f32) * scale).astype(bf16))
        scores = []
        for place, (ref, k) in enumerate(pieces):
            flags = ref[k, count : count + 1, :count]
            scores.append(scores_of(queries, ref[k, :count, at], flags, place == 0))
        top = jnp.max(scores[0], axis=-1, keepdims=True)
        for score in scores[1:]:
            top = jnp.maximum(top, jnp.max(score, axis=-1, keepdims=True))
        total, mixed = 0.0, 0.0
        for score, (ref, k) in zip(scores, pieces):
            grown = jnp.exp(score - top)
            total = total + jnp.sum(grown, axis=-1, keepdims=True)
            mixed = mixed + dot(grown.astype(bf16), ref[k, :count, past])
        mix_ref[:, at] = join_heads(mixed / total)
        logs = top + jnp.log(total)
        lse = jnp.where(lane == 2 * pair, logs[:count], lse)
        lse = jnp.where(lane == 2 * pair + 1, logs[count:], lse)
    lse_ref[...] = lse


def forward_rest(rows, mix, mod, layer, out, up, down):
    width = rows.shape[1]
    attn_low = mix.astype(bf16)
    branch1 = dot(attn_low, out[...])
    middle = rows + piece(mod, layer, 2, width) * branch1
    mlp_in = normed(middle, piece(mod, layer, 3, width), piece(mod, layer, 4, width))
    up_proj = dot(mlp_in, up[...])
    square, bent = gelu_parts(up_proj)
    gelu_low = (0.5 * up_proj * (1.0 + bent)).astype(bf16)
    branch2 = dot(gelu_low, down[...])
    result = middle + piece(mod, layer, 5, width) * branch2
    return attn_low, branch1, middle, mlp_in, up_proj, square, bent, gelu_low, branch2, result


def forward_kernel(layer, pairs, mod, rows, query, *refs):
    pair_refs, refs = refs[:pairs], refs[pairs:]
    out, up, down, qkv_next = refs[:4]
    mix, lse, branch1, middle, up_proj, branch2, stream, attn_next, query_next, pair_next = refs[4:]
    attend(query, pair_refs, mix, lse)
    kept = forward_rest(rows[...], mix[...], mod, layer, out, up, down)
    branch1[...], middle[...], up_proj[...], branch2[...] = kept[1], kept[2], kept[4], kept[8]
    stream[...] = kept[9]
    count = rows.shape[0]
    emit_qkv(kept[9], mod, layer + 1, qkv_next[...], attn_next, query_next, pair_next, pair_refs[0][0, count:])


def mlp_back(upstream, mod, layer, out, up, down, kept, d_mod, grads):
    attn_low, branch1, middle, mlp_in, up_proj, square, bent, gelu_low, branch2 = kept
    g_out, g_up, g_down, d_attn = grads
    width = upstream.shape[1]
    d_mod[2:3] = total_rows(upstream * branch2)
    d_branch2 = (piece(mod, layer, 5, width) * upstream).astype(bf16)
    g_down[...] = dot_rows(gelu_low, d_branch2).astype(bf16)
    d_gelu = dot_cols(d_branch2, down[...])
    slope = 0.5 * (1.0 + bent) + 0.5 * up_proj * (1.0 - bent * bent) * (
        gelu_scale * (1.0 + 3.0 * 0.044715 * square)
    )
    d_up = (d_gelu * slope).astype(bf16)
    g_up[...] = dot_rows(mlp_in, d_up).astype(bf16)
    d_mlp = dot_cols(d_up, up[...])
    normal, inverse = norm(middle)
    d_mod[0:1] = total_rows(d_mlp)
    d_mod[1:2] = total_rows(d_mlp * normal)
    d_mid = upstream + norm_back(normal, inverse, d_mlp * (1.0 + piece(mod, layer, 4, width)))
    d_mod[3:4] = total_rows(d_mid * branch1)
    d_mod[4:8] = jnp.zeros((4, width), f32)
    d_branch1 = (piece(mod, layer, 2, width) * d_mid).astype(bf16)
    g_out[...] = dot_rows(attn_low, d_branch1).astype(bf16)
    d_attn[...] = dot_cols(d_branch1, out[...]).astype(bf16)
    return d_mid


def turn_kernel(layer, pairs, mod, rows, query, *refs):
    pair_refs, refs = refs[:pairs], refs[pairs:]
    out, up, down, cot = refs[:4]
    mix, lse, output, d_mid, d_mod, g_out, g_up, g_down, d_attn = refs[4:]
    attend(query, pair_refs, mix, lse)
    kept = forward_rest(rows[...], mix[...], mod, layer, out, up, down)
    output[...] = kept[9].astype(bf16)
    d_mid[...] = mlp_back(cot[...], mod, layer, out, up, down, kept[:9], d_mod, (g_out, g_up, g_down, d_attn))


def attend_back_kernel(pairs, query_ref, mix_ref, lse_ref, grad_ref, *refs):
    pair_refs, d_query, d_pairs = refs[:pairs], refs[pairs], refs[pairs + 1 :]
    count, width = query_ref.shape
    pieces, d_pieces = pieces_of(pair_refs), pieces_of(d_pairs)
    scale = 1.0 / math.sqrt(width // HEADS)
    for pair in range(HEADS // 2):
        at = slice(pair * 128, (pair + 1) * 128)
        past = slice(width + pair * 128, width + (pair + 1) * 128)
        queries = split_heads((query_ref[:, at].astype(f32) * scale).astype(bf16))
        grad = grad_ref[:, at]
        grads = split_heads(grad)
        delta = jnp.sum(split_heads(grad.astype(f32) * mix_ref[:, at]), axis=-1, keepdims=True)
        logs = jnp.concatenate(
            [lse_ref[:, 2 * pair : 2 * pair + 1], lse_ref[:, 2 * pair + 1 : 2 * pair + 2]], axis=0
        )
        d_q = 0.0
        for place, ((ref, k), (d_ref, d_k)) in enumerate(zip(pieces, d_pieces)):
            keys, values = ref[k, :count, at], ref[k, :count, past]
            flags = ref[k, count : count + 1, :count]
            prob = jnp.exp(scores_of(queries, keys, flags, place == 0) - logs)
            d_prob = dot_cols(grads, values)
            d_score = (prob * (d_prob - delta)).astype(bf16)
            d_ref[d_k, :, past] = dot_rows(prob.astype(bf16), grads).astype(bf16)
            d_ref[d_k, :, at] = dot_rows(d_score, queries).astype(bf16)
            d_q = d_q + dot(d_score, keys)
        d_query[:, at] = (join_heads(d_q) * scale).astype(bf16)


def qkv_back(d_query, d_parts, attn_in, rows, mod, layer, weight, d_mid, g_qkv, d_mod):
    width = rows.shape[1]
    d_pair = d_parts[0][0].astype(f32)
    for part in d_parts[1:]:
        d_pair = d_pair + part[0].astype(f32)
    d_pair = d_pair.astype(bf16)
    g_qkv[:, :width] = dot_rows(attn_in[...], d_query[...]).astype(bf16)
    g_qkv[:, width:] = dot_rows(attn_in[...], d_pair).astype(bf16)
    d_in = dot_cols(d_query[...], weight[:, :width]) + dot_cols(d_pair, weight[:, width:])
    normal, inverse = norm(rows[...])
    d_mod[0:1] = total_rows(d_in)
    d_mod[1:2] = total_rows(d_in * normal)
    d_mod[2:8] = jnp.zeros((6, width), f32)
    return d_mid[...] + norm_back(normal, inverse, d_in * (1.0 + piece(mod, layer, 1, width)))


def qkv_back_kernel(layer, count, mod, d_query, *refs):
    parts, refs = refs[:count], refs[count:]
    attn_in, rows, weight, d_mid, upstream, g_qkv, d_mod = refs
    upstream[...] = qkv_back(
        d_query, parts, attn_in, rows, mod, layer, weight, d_mid, g_qkv, d_mod
    ).astype(upstream.dtype)


def mlp_back_kernel(layer, mod, upstream, mix, branch1, middle, up_proj, branch2, out, up, down, *refs):
    d_mid, d_mod = refs[:2]
    width = upstream.shape[1]
    mlp_in = normed(middle[...], piece(mod, layer, 3, width), piece(mod, layer, 4, width))
    square, bent = gelu_parts(up_proj[...])
    gelu_low = (0.5 * up_proj[...] * (1.0 + bent)).astype(bf16)
    kept = (mix[...].astype(bf16), branch1[...], middle[...], mlp_in, up_proj[...], square, bent, gelu_low, branch2[...])
    d_mid[...] = mlp_back(upstream[...], mod, layer, out, up, down, kept, d_mod, refs[2:])


def band_rows(array, bits):
    mine = lax.axis_index("lat") // bits.group
    rows = array.shape[0] // bits.items
    parts = []
    for far in range(bits.items):
        part = array[far * rows : (far + 1) * rows]
        if far:
            part = swap(part, ("lat", far * bits.group, bits.lat))
        parts.append(part)
    stacked = jnp.stack(parts)
    order = jnp.arange(bits.items, dtype=jnp.int32) ^ mine
    return jnp.take(stacked, order, axis=0)


def per_device(bits, patches, levels, lead_index, lead_table, ada, qkv, out, up, down, cotangent):
    layers = qkv.shape[0]
    band, width = patches.shape[1:]
    count = band * bits.items
    lat_at, batch_at = lax.axis_index("lat"), lax.axis_index("batch")
    mine = lat_at // bits.group
    pos = jnp.stack([lat_at, batch_at, mine]).astype(jnp.int32)
    shards = (qkv, out, up, down)
    weights = Weights(bits, shards, pos)

    load_shape = ((2 * band + flag_rows, width), bf16)
    if weights.tiled:
        rows, units = weights.rows, weights.units
        packed = call(
            partial(pack_kernel, down.shape[1] // rows, bits.items),
            [((rows, units), bf16)] * 2 + [((2 * rows, units), bf16)] * 2 + [load_shape] * bits.items,
            [qkv, out, up, down, patches, levels, cotangent],
            pos,
            name="pack",
        )
        firsts, seconds, loads = packed[:2], packed[2:4], packed[4:]
    else:
        both = [pack_shards(shards, layer) for layer in range(layers)]
        firsts, seconds = [pair[0] for pair in both], [pair[1] for pair in both]
        loads = call(partial(load_kernel, bits.items), [load_shape] * bits.items, [patches, levels, cotangent], pos)
    loads = [loads[0]] + [
        swap(loads[far], ("lat", far * bits.group, bits.lat)) for far in range(1, bits.items)
    ]

    table_rows, lat_cols = lead_table.shape
    lead_row = jnp.broadcast_to(lead_index.astype(f32)[None], (table_rows, bits.items))
    lead_row = jnp.concatenate([lead_table.astype(f32), lead_row], axis=1)
    got = gather(lead_row, bits.bs)
    batch_far = jnp.arange(bits.batch, dtype=jnp.int32)
    row_ids = ((batch_at ^ batch_far)[:, None] * table_rows + jnp.arange(table_rows)[None]).reshape(-1)
    table = got[:, :, :lat_cols].reshape(-1, lat_cols)
    leads = got[:, 0, lat_cols:].reshape(-1)
    hot = (leads[:, None] == row_ids[None, :].astype(f32)).astype(f32)
    embed = jnp.dot(hot, table, precision=highest)
    cond = jax.nn.silu(embed).astype(bf16)
    part = jnp.stack([dot(cond, ada[layer]) for layer in range(layers)], axis=1)
    columns = part.shape[-1]
    part = part.reshape(bits.batch, bits.items, layers, columns)
    part = jnp.take(part, mine ^ jnp.arange(bits.items, dtype=jnp.int32), axis=1)
    part = part.transpose(1, 0, 2, 3)
    part = scatter(part, bits.item)
    for stage in bits.zs + [bits.core]:
        part = part + swap(part, stage)
    part = spread(part, bits.bs)
    part = jnp.take(part, batch_at ^ batch_far, axis=0)
    mod = part.transpose(1, 0, 2).reshape(layers, 6 * width)

    whole = [weights.first(firsts[0]) + weights.second(seconds[0])]
    whole += [weights.first(firsts[layer]) + weights.second(seconds[layer]) for layer in range(1, layers)]

    rows_kind, low_kind = ((count, width), f32), ((count, width), bf16)
    pair_kind = ((1, count + flag_rows, 2 * width), bf16)
    lse_kind, mod_kind = ((count, 128), f32), ((8, width), f32)
    stream, cot, attn_in, query, pair = call(
        partial(start_kernel, bits.items),
        [rows_kind, rows_kind, low_kind, low_kind, pair_kind],
        [mod, whole[0][0]] + list(loads),
        name="start",
    )
    saved = []
    for layer in range(layers):
        w_qkv, w_out, w_up, w_down = whole[layer]
        chip = [pair]
        for stage in bits.zs:
            joined = chip[0] if len(chip) == 1 else jnp.concatenate(chip, axis=0)
            chip = chip + [swap(joined, stage)]
        pairs = chip + [swap(part, bits.core) for part in chip]
        given = [mod, stream, query] + pairs + [w_out, w_up, w_down]
        if layer + 1 < layers:
            wide = ((count, w_up.shape[1]), f32)
            mix, lse, branch1, middle, up_proj, branch2, result, attn_next, query_next, pair = call(
                partial(forward_kernel, layer, len(pairs)),
                [rows_kind, lse_kind, rows_kind, rows_kind, wide, rows_kind, rows_kind, low_kind, low_kind, pair_kind],
                given + [whole[layer + 1][0]],
                name="forward",
            )
            saved.append((stream, attn_in, query, pairs, mix, lse, branch1, middle, up_proj, branch2))
            stream, attn_in, query = result, attn_next, query_next
    square_kind = ((width, width), bf16)
    grad_kinds = [square_kind, (w_up.shape, bf16), (w_down.shape, bf16), low_kind]
    mix, lse, output, d_mid, d_mlp_mod, g_out, g_up, g_down, d_attn = call(
        partial(turn_kernel, layers - 1, len(pairs)),
        [rows_kind, lse_kind, low_kind, rows_kind, mod_kind] + grad_kinds,
        given + [cot],
        name="turn",
    )
    saved.append((stream, attn_in, query, pairs, mix, lse))
    output = band_rows(output, bits)

    grads, mods = [None] * layers, [None] * layers
    for layer in reversed(range(layers)):
        stream, attn_in, query, pairs, mix, lse = saved[layer][:6]
        second = weights.second_sum(g_up, g_down)
        backs = call(
            partial(attend_back_kernel, len(pairs)),
            [low_kind] + [((p.shape[0], count, 2 * width), bf16) for p in pairs],
            [query, mix, lse, d_attn] + pairs,
            name="attend_back",
        )
        d_query, d_chip, d_core = backs[0], backs[1 : 1 + len(pairs) // 2], backs[1 + len(pairs) // 2 :]
        got = [swap(part, bits.core) for part in d_core]
        parts = [d_chip[0], got[0]]
        if bits.zs:
            rest = [
                call(add_kernel, [(p.shape, bf16)], [p, q], name="add_pairs")[0]
                for p, q in zip(d_chip[1:], got[1:])
            ]
            held = [rest[0]] if len(rest) == 1 else rest
            for place in reversed(range(len(bits.zs))):
                back = swap(held[place], bits.zs[place])
                if place == 0:
                    parts.append(back)
                else:
                    parts.append(back[:1])
                    at = 1
                    for near in range(place):
                        size = held[near].shape[0]
                        held[near] = held[near] + back[at : at + size]
                        at += size
        upstream, g_qkv, d_qkv_mod = call(
            partial(qkv_back_kernel, layer, len(parts)),
            [rows_kind if layer else low_kind, ((width, 3 * width), bf16), mod_kind],
            [mod, d_query] + parts + [attn_in, stream, whole[layer][0], d_mid],
            name="qkv_back",
        )
        mods[layer] = jnp.concatenate([d_qkv_mod[0:2], d_mlp_mod[3:4], d_mlp_mod[0:3]], axis=0)
        grads[layer] = (weights.first_sum(g_qkv, g_out), second)
        if layer:
            w_out, w_up, w_down = whole[layer - 1][1:]
            mix, lse, branch1, middle, up_proj, branch2 = saved[layer - 1][4:]
            d_mid, d_mlp_mod, g_out, g_up, g_down, d_attn = call(
                partial(mlp_back_kernel, layer - 1),
                [rows_kind, mod_kind] + grad_kinds,
                [mod, upstream, mix, branch1, middle, up_proj, branch2, w_out, w_up, w_down],
                name="mlp_back",
            )
    patches_grad = band_rows(upstream, bits)

    d_mod = jnp.stack(mods)
    for stage in bits.zs + [bits.core]:
        d_mod = d_mod + swap(d_mod, stage)
    d_mod = gather(d_mod, bits.item)
    d_mod = d_mod.reshape(bits.items, layers, bits.batch, columns).transpose(2, 0, 1, 3)
    d_mod = jnp.take(d_mod, batch_at ^ batch_far, axis=0)
    d_mod = spread(d_mod, bits.bs)
    d_mod = jnp.take(d_mod, mine ^ jnp.arange(bits.items, dtype=jnp.int32), axis=1)
    d_mod = d_mod.reshape(-1, layers, columns)
    ada_grad = jnp.stack(
        [
            lax.dot_general(cond.astype(f32), d_mod[:, layer], (((0,), (0,)), ((), ())), precision=highest)
            for layer in range(layers)
        ]
    )
    d_cond = sum(
        lax.dot_general(d_mod[:, layer], ada[layer].astype(f32), (((1,), (1,)), ((), ())), precision=highest)
        for layer in range(layers)
    )
    d_embed = jax.vjp(jax.nn.silu, embed)[1](d_cond)[0]
    table_part = lax.dot_general(hot, d_embed, (((0,), (0,)), ((), ())), precision=highest)
    table_grad = scatter(table_part.reshape(bits.batch, table_rows, lat_cols), bits.bs)

    rows, cols, thin = weights.rows, weights.columns, weights.thin
    lows = [
        jnp.concatenate([pair[1][rows:, k * thin : (k + 1) * thin] for k in range(weights.units // thin)], axis=0)
        for pair in grads
    ]
    return (
        output,
        patches_grad,
        table_grad,
        ada_grad,
        jnp.stack([pair[0][:, :cols] for pair in grads]),
        jnp.stack([pair[0][:, cols:] for pair in grads]),
        jnp.stack([pair[1][:rows] for pair in grads]),
        jnp.stack(lows),
    )


def solution(mesh):
    batch, lat = mesh.shape["batch"], mesh.shape["lat"]

    def run(*arrays):
        bits = Bits(batch, lat, arrays[0].shape[0] // batch)
        Place.near = arrays[0].shape[1] <= 1024
        rows = P("batch", "lat", None)
        weight = P(None, "lat", "batch")
        return jax.shard_map(
            lambda *pieces: per_device(bits, *pieces),
            mesh=mesh,
            in_specs=(rows, P("batch", "lat"), P("batch"), P("batch", "lat"), weight, weight, weight, weight, weight, rows),
            out_specs=(rows, rows, P("batch", "lat"), weight, weight, weight, weight, weight),
            check_vma=False,
        )(*arrays)

    return run
```
